256 devices in a mesh: layer: 16 (over x_lo, z), tok: 16 (over y, x_hi, core).
Axes of the slice: x: 4 (x_hi: 2, x_lo: 2; x = x_hi * 2 + x_lo), y: 4, z: 8, core: 2. Of those that a mesh axis runs over, the one named last changes fastest.
Arguments:
- acts: bfloat16 [16, 512, 2048], P('layer', 'tok'), may hold values from -6 to 6
- w_enc: bfloat16 [16, 2048, 1024], P('layer', 'tok'), may hold values from -0.125 to 0.125
- b_enc: float32 [16, 1024], P('layer'), may hold values from -0.5 to 0.5
- w_dec: bfloat16 [16, 16, 1024, 2048], P('layer', None, None, 'tok'), may hold values from -0.046875 to 0.046875
- targets: bfloat16 [16, 512, 2048], P('layer', None, 'tok'), may hold values from -6 to 6
Outputs:
- code_grad: float32 [16, 512, 1024], P('layer', 'tok')
- dec_grad: bfloat16 [16, 16, 1024, 2048], P('layer', None, None, 'tok')
The draws below stay inside these ranges and needn't reach their ends.
All inputs are finite; a program needn't handle non-finite values.
Results may differ from the reference program's by a relative error of at most 0.0034.
Values may be sent and summed in bfloat16 or wider, within the bound.
No kernel may reach another device: no remote copies, remote signals or barrier semaphores. Data moves between devices by JAX's collectives and lax.ppermute only.
A program may use at most 64 MiB of HBM per device.

```python
import jax
import jax.numpy as jnp
from jax import lax

D = 2048
F = 1024
TOKENS = 512
LAYERS = 16


def block_levels(key, shape, shards, low, top_value):
    level = 1.0
    for position, parts in shards:
        steps = jax.random.uniform(jax.random.fold_in(jax.random.fold_in(key, 6), position), (parts,), jnp.float32, low / len(shards), top_value / len(shards))
        level = level * jnp.repeat(jnp.exp(steps), shape[position] // parts).reshape((-1,) + (1,) * (len(shape) - 1 - position))
    return level


def bell_draw(own_key, shape, width, limit, shards=(), dtype=jnp.bfloat16):
    gain = block_levels(own_key, shape, shards, -0.22, 0.18) if shards else 1.0
    result = jax.random.normal(own_key, shape, jnp.float32) * width * gain
    return jnp.minimum(jnp.maximum(result, -limit), limit).astype(dtype)


def setup_inputs(seed: int = 0) -> dict:
    streams_of = jax.random.split(jax.random.key(seed), 6)
    return {
        "acts": bell_draw(streams_of[0], (LAYERS, TOKENS, D), 1.0, 6.0, ((0, 16), (1, 16))),
        "w_enc": bell_draw(streams_of[1], (LAYERS, D, F), D ** -0.5, 0.125, ((0, 16), (1, 16))),
        "b_enc": jnp.clip(jax.random.uniform(streams_of[2], (LAYERS, F), jnp.float32, -0.5, 0.5) * block_levels(streams_of[2], (LAYERS, F), ((0, 16),), -0.4, 0.0), -0.5, 0.5),
        "w_dec": bell_draw(streams_of[3], (LAYERS, LAYERS, F, D), (F * LAYERS) ** -0.5, 0.046875, ((0, 16), (3, 16))),
        "targets": bell_draw(streams_of[4], (LAYERS, TOKENS, D), 1.0, 6.0, ((0, 16), (2, 16))),
    }


def reference(acts, w_enc, b_enc, w_dec, targets):
    layers = w_dec.shape[0]
    layer_order = jnp.arange(layers)
    pair_live = layer_order[:, None] <= layer_order[None, :]

    def encode(inputs):
        source, weight, bias = inputs
        preact = jnp.dot(source, weight, preferred_element_type=jnp.float32) + bias
        return jnp.maximum(preact, 0.0).astype(jnp.bfloat16)

    feature_codes = lax.map(encode, (acts, w_enc, b_enc))

    def forward(total, inputs):
        source, dec_slabs, pair_keep = inputs
        masked = jnp.where(pair_keep[:, None, None], dec_slabs.astype(jnp.float32), 0.0)
        product = jnp.einsum("tf,jfd->jtd", source.astype(jnp.float32), masked, precision=lax.Precision.HIGHEST)
        return total + product, None

    empty_sum = jnp.zeros((layers, TOKENS, D), jnp.float32)
    rebuilt, _ = lax.scan(forward, empty_sum, (feature_codes, w_dec, pair_live))
    errors_wide = rebuilt - targets.astype(jnp.float32)

    def backward(inputs):
        source, dec_slabs, pair_keep = inputs
        masked = jnp.where(pair_keep[:, None, None], dec_slabs.astype(jnp.float32), 0.0)
        weight_grad = jnp.einsum("tf,jtd->jfd", source.astype(jnp.float32), errors_wide, precision=lax.Precision.HIGHEST)
        weight_grad = jnp.where(pair_keep[:, None, None], weight_grad, 0.0).astype(jnp.bfloat16)
        code_part = jnp.einsum("jtd,jfd->tf", errors_wide, masked, precision=lax.Precision.HIGHEST)
        return code_part, weight_grad

    code_grad, dec_grad = lax.map(backward, (feature_codes, w_dec, pair_live))
    return code_grad, dec_grad
```

```python
import functools

import jax
import jax.numpy as jnp
from jax import lax
from jax.experimental import pallas as pl
from jax.experimental.pallas import tpu as pltpu
from jax.sharding import PartitionSpec as P

BF = jnp.bfloat16
F32 = jnp.float32
AXES = ("layer", "tok")
NL, NT, NZ = 16, 16, 8


def _layer_perm(fn):
    return [(l * NT + t, fn(l) * NT + t) for l in range(NL) for t in range(NT)]


def _tok_perm(fn):
    return [(l * NT + t, l * NT + fn(t)) for l in range(NL) for t in range(NT)]


Z_UP = _layer_perm(lambda l: (l // NZ) * NZ + (l + 1) % NZ)
Z_DOWN = _layer_perm(lambda l: (l // NZ) * NZ + (l - 1) % NZ)
X_SWAP = _layer_perm(lambda l: l ^ NZ)
CORE_SWAP = _tok_perm(lambda t: t ^ 1)
XHI_SWAP = _tok_perm(lambda t: t ^ 2)

G_PLANE = [[y * 4 + q for q in range(4)] for y in range(4)]
G_Y = [[y * 4 + q for y in range(4)] for q in range(4)]
G_CHIP = [[y * 4 + xh * 2 + c for xh in range(2) for y in range(4)] for c in range(2)]


def permute(x, pairs):
    return lax.ppermute(x, AXES, pairs)


def swap_blocks(x, groups):
    return lax.all_to_all(x, "tok", 0, 0, axis_index_groups=groups)


def spread(x, groups):
    return swap_blocks(jnp.broadcast_to(x[None], (len(groups[0]),) + x.shape), groups)


def call(kernel, grid, in_specs, out_specs, out_shape, scratch, flops, nbytes, aliases=None):
    return pl.pallas_call(
        kernel,
        grid_spec=pltpu.PrefetchScalarGridSpec(
            num_scalar_prefetch=1,
            grid=grid,
            in_specs=in_specs,
            out_specs=out_specs,
            scratch_shapes=scratch,
        ),
        out_shape=out_shape,
        input_output_aliases=aliases or {},
        cost_estimate=pl.CostEstimate(flops=flops, bytes_accessed=nbytes, transcendentals=0),
        compiler_params=pltpu.CompilerParams(vmem_limit_bytes=40 << 20),
    )


def whole(shape):
    return pl.BlockSpec(shape, lambda *_: (0,) * len(shape))


def encode_kernel(pos, a0, a1, a2, w_ref, b_ref, out_ref, acts):
    q = pos[2]
    for r, part in enumerate((a0, a1, a2.at[0], a2.at[1])):
        acts[pl.ds(pl.multiple_of((q ^ r) * 32, 32), 32), :] = part[...]
    pre = jnp.dot(acts[...], w_ref[...], preferred_element_type=F32)
    out_ref[...] = jnp.maximum(pre + b_ref[...], 0.0).astype(BF)


def encode(pos, a0, a1, a2, w, b):
    return call(
        encode_kernel,
        (1,),
        [
            whole(a0.shape),
            whole(a1.shape),
            whole(a2.shape),
            whole(w.shape),
            pl.BlockSpec((1, 256), lambda i, pos: (0, pos[2])),
        ],
        whole((128, 256)),
        jax.ShapeDtypeStruct((128, 256), BF),
        [pltpu.VMEM((128, 2048), BF)],
        2 * 128 * 2048 * 256,
        2 << 20,
    )(pos, a0, a1, a2, w, b)


def project_kernel(dists, pos, own, other, w_ref, out_ref, *rest):
    codes = rest[-1]
    step = pl.program_id(0)
    layer, c = pos[0], pos[1]
    x, z = layer // NZ, layer % NZ

    @pl.when(step == 0)
    def _():
        for xh in range(2):
            codes[:, pl.ds(pl.multiple_of((xh * 2 + c) * 256, 256), 256)] = own[xh]
            codes[:, pl.ds(pl.multiple_of((xh * 2 + 1 - c) * 256, 256), 256)] = other[xh]
        if len(rest) > 1:
            rest[0][...] = codes[...].T

    target = lax.rem(z + step + dists, NZ)
    live = NZ + target >= layer

    @pl.when(live)
    def _():
        w = jnp.concatenate([w_ref[0, 0], w_ref[1, 0]], axis=1)
        prod = jnp.dot(codes[...], w, preferred_element_type=F32)
        out_ref[0, x] = jnp.where(target >= layer, prod[:, :128], 0.0).astype(out_ref.dtype)
        out_ref[0, 1 - x] = prod[:, 128:].astype(out_ref.dtype)

    @pl.when(jnp.logical_not(live))
    def _():
        out_ref[...] = jnp.zeros_like(out_ref)


def project(pos, own, other, w, first, count, transposed):
    outs = [jax.ShapeDtypeStruct((count, 2, 512, 128), F32)]
    specs = [pl.BlockSpec((1, 2, 512, 128), lambda i, pos: (i, 0, 0, 0))]
    if transposed:
        outs.append(jax.ShapeDtypeStruct((1024, 512), BF))
        specs.append(whole((1024, 512)))
    return call(
        functools.partial(project_kernel, first),
        (count,),
        [
            whole((2, 512, 256)),
            whole((2, 512, 256)),
            pl.BlockSpec(
                (2, 1, 1024, 128),
                lambda i, pos: (0, lax.rem(pos[0] + i + first, NZ), 0, 0),
            ),
        ],
        specs,
        outs,
        [pltpu.VMEM((512, 1024), BF)],
        count * 2 * 512 * 1024 * 256,
        count << 20,
    )(pos, own, other, w)


def backprop_kernel(dists, first_call, pos, *refs):
    n = len(dists)
    errs, rest = refs[:n], refs[n:]
    codes_t, w_ref = rest[0], rest[1]
    rest = rest[2:] if first_call else rest[4:]
    dec_ref, acc_ref, err = rest
    if not first_call:
        acc_in = refs[n + 3]
    step = pl.program_id(0)
    layer = pos[0]
    x, z = layer // NZ, layer % NZ

    if first_call:

        @pl.when(step == 0)
        def _():
            acc_ref[...] = jnp.zeros_like(acc_ref)

    else:

        @pl.when(step == 0)
        def _():
            acc_ref[...] = acc_in[...]

    target = z
    for k, d in enumerate(dists):
        target = jnp.where(step == k, lax.rem(z + d, NZ), target)
    live = NZ + target >= layer

    @pl.when(live)
    def _():
        for k in range(n):

            @pl.when(step == k)
            def _(k=k):
                zero = jnp.zeros((512, 128), BF)
                err[:, :128] = jnp.where(target >= layer, errs[k][x], zero)
                err[:, 128:] = errs[k][1 - x]

        e = err[...]
        grad = jnp.dot(codes_t[...], e, preferred_element_type=F32)
        dec_ref[0, 0] = grad[:, :128].astype(BF)
        dec_ref[1, 0] = grad[:, 128:].astype(BF)
        w = jnp.concatenate([w_ref[0, 0], w_ref[1, 0]], axis=1)
        acc_ref[...] += lax.dot_general(
            e, w, (((1,), (1,)), ((), ())), preferred_element_type=F32
        )

    @pl.when(jnp.logical_not(live))
    def _():
        dec_ref[...] = jnp.zeros_like(dec_ref)


def backprop(pos, errs, dists, codes_t, w, carry=None):
    n = len(dists)

    def z_map(i, pos):
        target = pos[0]
        for k, d in enumerate(dists):
            target = jnp.where(i == k, pos[0] + d, target)
        return (0, lax.rem(target, NZ), 0, 0)

    blocks = pl.BlockSpec((2, 1, 1024, 128), z_map)
    specs = [whole((2, 512, 128))] * n + [whole((1024, 512)), blocks]
    args = [pos, *errs, codes_t, w]
    aliases = {}
    if carry is not None:
        specs += [pl.BlockSpec(memory_space=pl.ANY), whole((512, 1024))]
        args += list(carry)
        aliases = {n + 3: 0}
    return call(
        functools.partial(backprop_kernel, dists, carry is None),
        (n,),
        specs,
        [blocks, whole((512, 1024))],
        [
            jax.ShapeDtypeStruct((2, NZ, 1024, 128), BF),
            jax.ShapeDtypeStruct((512, 1024), F32),
        ],
        [pltpu.VMEM((512, 256), BF)],
        n * 4 * 512 * 1024 * 256,
        n << 20,
        aliases,
    )(*args)


def local(acts, w_enc, b_enc, w_dec, targets):
    layer = lax.axis_index("layer")
    tok = lax.axis_index("tok")
    pos = jnp.stack([layer, tok % 2, tok % 4]).astype(jnp.int32)

    a0 = acts[0]
    a1 = permute(a0, CORE_SWAP)
    a2 = permute(jnp.stack([a0, a1]), XHI_SWAP)
    w_cols = jnp.transpose(w_enc[0].reshape(128, 4, 256), (1, 0, 2))
    w_rows = swap_blocks(w_cols, G_PLANE).reshape(512, 256)
    w_full = spread(w_rows, G_Y).reshape(2048, 256)
    block = encode(pos, a0, a1, a2, w_full, b_enc)
    own = spread(block, G_CHIP).reshape(2, 512, 256)
    other = permute(own, CORE_SWAP)

    w = w_dec[0].reshape(2, NZ, 1024, 128)
    (far,) = project(pos, own, other, w, 4, 1, False)
    near, codes_t = project(pos, own, other, w, 5, 7, True)
    parts = {d: near[d - 5] for d in (5, 6, 7)}
    parts.update({d: near[d + 3] for d in (0, 1, 2, 3)})
    up = permute(far[0, 0].astype(BF), Z_UP).astype(F32)
    down = permute(far[0, 1].astype(BF), Z_DOWN).astype(F32)
    up = jnp.stack([parts[3][0] + up, parts[3][1]])
    down = jnp.stack([parts[5][0], parts[5][1] + down])
    for hop in (2, 1, 0):
        up = permute(up.astype(BF), Z_UP).astype(F32)
        down = permute(down.astype(BF), Z_DOWN).astype(F32)
        if hop:
            up = up + parts[hop]
            down = down + parts[NZ - hop]
    total = parts[0] + up + down
    cross = permute(total[1].astype(BF), X_SWAP).astype(F32)
    err = (total[0] + cross - targets[0].astype(F32)).astype(BF)

    pair = jnp.stack([err, permute(err, X_SWAP)])
    ups, downs = [pair], [pair]
    for _ in range(3):
        ups.append(permute(ups[-1], Z_UP))
        downs.append(permute(downs[-1], Z_DOWN))
    opposite = jnp.stack(
        [permute(ups[-1][0], Z_UP), permute(downs[-1][1], Z_DOWN)]
    )
    carry = backprop(
        pos,
        [pair, ups[1], downs[1], ups[2], downs[2]],
        (0, 7, 1, 6, 2),
        codes_t,
        w,
    )
    dec_grad, partial = backprop(
        pos, [ups[3], downs[3], opposite], (5, 3, 4), codes_t, w, carry
    )

    halves = partial.reshape(8, 2, 32, 1024)
    core = tok % 2
    keep = lax.dynamic_index_in_dim(halves, core, 1, keepdims=False)
    give = lax.dynamic_index_in_dim(halves, 1 - core, 1, keepdims=False)
    chip = keep + permute(give, CORE_SWAP)
    chip = chip.reshape(4, 2, 32, 1024).transpose(1, 0, 2, 3).reshape(8, 32, 1024)
    shares = swap_blocks(chip.astype(BF), G_CHIP).astype(F32)
    code_grad = jnp.sum(shares, axis=0)
    return code_grad[None], dec_grad.reshape(1, NL, 1024, 128)


def solution(mesh):
    return jax.shard_map(
        local,
        mesh=mesh,
        in_specs=(
            P("layer", "tok", None),
            P("layer", "tok", None),
            P("layer", None),
            P("layer", None, None, "tok"),
            P("layer", None, "tok"),
        ),
        out_specs=(P("layer", "tok", None), P("layer", None, None, "tok")),
        check_vma=False,
    )
```

```python
import functools

import jax
import jax.numpy as jnp
from jax import lax
from jax.experimental import pallas as pl
from jax.experimental.pallas import tpu as pltpu
from jax.sharding import PartitionSpec as P


BF = jnp.bfloat16
F32 = jnp.float32
AXES = ("layer", "tok")
NL, NT, NZ = 16, 16, 8


def _layer_perm(fn):
    return [(l * NT + t, fn(l) * NT + t) for l in range(NL) for t in range(NT)]


def _tok_perm(fn):
    return [(l * NT + t, l * NT + fn(t)) for l in range(NL) for t in range(NT)]


Z_UP = _layer_perm(lambda l: (l // NZ) * NZ + (l + 1) % NZ)
Z_DOWN = _layer_perm(lambda l: (l // NZ) * NZ + (l - 1) % NZ)
X_SWAP = _layer_perm(lambda l: l ^ NZ)
CORE_SWAP = _tok_perm(lambda t: t ^ 1)
XHI_SWAP = _tok_perm(lambda t: t ^ 2)

G_OUT = [[y * 4 + xh * 2 + c for y in range(4) for xh in range(2)] for c in range(2)]
G_CHIP = [[y * 4 + xh * 2 + c for xh in range(2) for y in range(4)] for c in range(2)]


def permute(x, pairs):
    return lax.ppermute(x, AXES, pairs)


def swap_blocks(x, groups):
    return lax.all_to_all(x, "tok", 0, 0, axis_index_groups=groups)


def call(kernel, in_specs, outs, scratch, flops, nbytes, aliases=None, room=16):
    return pl.pallas_call(
        kernel,
        in_specs=in_specs,
        out_specs=[o[1] for o in outs],
        out_shape=[o[0] for o in outs],
        scratch_shapes=scratch,
        input_output_aliases=aliases or {},
        cost_estimate=pl.CostEstimate(flops=flops, bytes_accessed=nbytes, transcendentals=0),
        compiler_params=pltpu.CompilerParams(vmem_limit_bytes=room << 20),
    )


SMEM = pl.BlockSpec(memory_space=pltpu.SMEM)
VMEM = pl.BlockSpec(memory_space=pltpu.VMEM)
HBM = pl.BlockSpec(memory_space=pltpu.HBM)


def in_vmem(shape, dtype):
    return (jax.ShapeDtypeStruct(shape, dtype), VMEM)


def in_hbm(shape, dtype):
    return (jax.ShapeDtypeStruct(shape, dtype), HBM)


def columns_kernel(w_ref, out_ref):
    for t in range(NT):
        q = t % 4
        out_ref[t] = w_ref[:, q * 256 : (q + 1) * 256]


def columns(w):
    return call(columns_kernel, [VMEM], [in_vmem((NT, 128, 256), BF)], [], 0, 5 << 18)(w)[0]


def encode_kernel(pos, a0, a1, a2, a3, w_ref, b_ref, out_ref, acts):
    q = pos[2]
    for r, part in enumerate((a0, a1, a2, a3)):
        acts[pl.ds(pl.multiple_of((q ^ r) * 32, 32), 32), :] = part[...]
    pre = jnp.dot(acts[...], w_ref[...], preferred_element_type=F32)
    bias = b_ref[:, pl.ds(pl.multiple_of(q * 256, 256), 256)]
    codes = jnp.maximum(pre + bias, 0.0).astype(BF)
    for k in range(8):
        out_ref[k] = codes


def encode(pos, a0, a1, a2, a3, w, b):
    return call(
        encode_kernel,
        [SMEM] + [VMEM] * 6,
        [in_vmem((8, 128, 256), BF)],
        [pltpu.VMEM((128, 2048), BF)],
        2 * 128 * 2048 * 256,
        2 << 20,
    )(pos, a0, a1, a2, a3, w, b)[0]


def project_kernel(first, count, pos, own, other, w_hbm, out_ref, *rest):
    codes, slabs, sems = rest[-3:]
    layer, c = pos[0], pos[1]
    x, z = layer // NZ, layer % NZ

    def fetch(k):
        target = lax.rem(z + k + first, NZ)
        return pltpu.make_async_copy(w_hbm.at[:, target], slabs.at[k], sems.at[k])

    def start(k, _):
        fetch(k).start()
        return 0

    lax.fori_loop(0, count, start, 0)
    for xh in range(2):
        codes[:, pl.ds(pl.multiple_of((xh * 2 + c) * 256, 256), 256)] = own[xh]
        codes[:, pl.ds(pl.multiple_of((xh * 2 + 1 - c) * 256, 256), 256)] = other[xh]

    def advance(k, _):
        target = lax.rem(z + k + first, NZ)
        live = NZ + target >= layer
        fetch(k).wait()

        @pl.when(live)
        def _():
            w = jnp.concatenate([slabs[k, 0], slabs[k, 1]], axis=1)
            prod = jnp.dot(codes[...], w, preferred_element_type=F32)
            out_ref[k, x] = jnp.where(target >= layer, prod[:, :128], 0.0).astype(out_ref.dtype)
            out_ref[k, 1 - x] = prod[:, 128:].astype(out_ref.dtype)

        @pl.when(jnp.logical_not(live))
        def _():
            out_ref[k] = jnp.zeros((2, 512, 128), out_ref.dtype)

        return 0

    lax.fori_loop(0, count, advance, 0)
    if len(rest) > 3:
        rest[0][...] = codes[...].T


def project(pos, own, other, w, first, count, dtype, transposed):
    outs = [in_vmem((count, 2, 512, 128), dtype)]
    if transposed:
        outs.append(in_vmem((1024, 512), BF))
    return call(
        functools.partial(project_kernel, first, count),
        [SMEM, VMEM, VMEM, HBM],
        outs,
        [
            pltpu.VMEM((512, 1024), BF),
            pltpu.VMEM((count, 2, 1024, 128), BF),
            pltpu.SemaphoreType.DMA((count,)),
        ],
        count * 2 * 512 * 1024 * 256,
        count << 20,
    )(pos, own, other, w)


def backprop_kernel(dists, first_call, pos, *refs):
    count = len(refs) - (9 if first_call else 11)
    errs = refs[:count]
    codes_t, w_hbm = refs[count], refs[count + 1]
    dec_hbm, acc_ref, err, slabs, grads, in_sems, out_sems = refs[-7:]
    layer = pos[0]
    x, z = layer // NZ, layer % NZ
    targets = [lax.rem(z + d, NZ) for d in dists]
    fetches = [
        pltpu.make_async_copy(w_hbm.at[:, t], slabs.at[k], in_sems.at[k])
        for k, t in enumerate(targets)
    ]
    stores = [
        pltpu.make_async_copy(grads.at[k], dec_hbm.at[:, t], out_sems.at[k])
        for k, t in enumerate(targets)
    ]
    for fetch in fetches:
        fetch.start()
    if first_call:
        acc_ref[...] = jnp.zeros_like(acc_ref)
    for k, target in enumerate(targets):
        live = NZ + target >= layer
        fetches[k].wait()

        @pl.when(live)
        def _(k=k, target=target):
            zero = jnp.zeros((512, 128), BF)
            if count > len(dists):
                blocks = errs[0][...], errs[1][...]
                err[:, :128] = jnp.where(target >= layer, jnp.where(x == 0, *blocks), zero)
                err[:, 128:] = jnp.where(x == 0, *blocks[::-1])
            else:
                err[:, :128] = jnp.where(target >= layer, errs[k][x], zero)
                err[:, 128:] = errs[k][1 - x]
            e = err[...]
            grad = jnp.dot(codes_t[...], e, preferred_element_type=F32)
            grads[k, 0] = grad[:, :128].astype(BF)
            grads[k, 1] = grad[:, 128:].astype(BF)
            w = jnp.concatenate([slabs[k, 0], slabs[k, 1]], axis=1)
            acc_ref[...] += lax.dot_general(
                e, w, (((1,), (1,)), ((), ())), preferred_element_type=F32
            )

        @pl.when(jnp.logical_not(live))
        def _(k=k):
            grads[k] = jnp.zeros((2, 1024, 128), BF)

        stores[k].start()
    for store in stores:
        store.wait()


def backprop(pos, errs, dists, codes_t, w, carry=None):
    n, count = len(dists), len(errs)
    specs = [SMEM] + [VMEM] * count + [VMEM, HBM]
    args = [pos, *errs, codes_t, w]
    aliases = {}
    if carry is not None:
        specs += [HBM, VMEM]
        args += list(carry)
        aliases = {count + 3: 0, count + 4: 1}
    return call(
        functools.partial(backprop_kernel, dists, carry is None),
        specs,
        [in_hbm((2, NZ, 1024, 128), BF), in_vmem((512, 1024), F32)],
        [
            pltpu.VMEM((512, 256), BF),
            pltpu.VMEM((n, 2, 1024, 128), BF),
            pltpu.VMEM((n, 2, 1024, 128), BF),
            pltpu.SemaphoreType.DMA((n,)),
            pltpu.SemaphoreType.DMA((n,)),
        ],
        n * 4 * 512 * 1024 * 256,
        n << 20,
        aliases,
    )(*args)


def body(acts, w_enc, b_enc, w_dec, targets):
    layer = lax.axis_index("layer")
    tok = lax.axis_index("tok")
    pos = jnp.stack([layer, tok % 2, tok % 4]).astype(jnp.int32)

    a0 = acts[0]
    a1 = permute(a0, CORE_SWAP)
    a2 = permute(a0, XHI_SWAP)
    a3 = permute(a2, CORE_SWAP)
    w_full = swap_blocks(columns(w_enc[0]), None).reshape(2048, 256)
    block = encode(pos, a0, a1, a2, a3, w_full, b_enc)
    own = swap_blocks(block, G_CHIP).reshape(2, 512, 256)
    other = permute(own, CORE_SWAP)

    w = pltpu.with_memory_space_constraint(w_dec[0].reshape(2, NZ, 1024, 128), pltpu.HBM)
    (far,) = project(pos, own, other, w, 4, 1, BF, False)
    near, codes_t = project(pos, own, other, w, 5, 7, F32, True)
    parts = {d: near[d - 5] for d in (5, 6, 7)}
    parts.update({d: near[d + 3] for d in (0, 1, 2, 3)})
    up = permute(far[0, 0], Z_UP).astype(F32)
    down = permute(far[0, 1], Z_DOWN).astype(F32)
    up = jnp.stack([parts[3][0] + up, parts[3][1]])
    down = jnp.stack([parts[5][0], parts[5][1] + down])
    for hop in (2, 1, 0):
        up = permute(up.astype(BF), Z_UP).astype(F32)
        down = permute(down.astype(BF), Z_DOWN).astype(F32)
        if hop:
            up = up + parts[hop]
            down = down + parts[NZ - hop]
    total = parts[0] + up + down
    cross = permute(total[1].astype(BF), X_SWAP).astype(F32)
    err = (total[0] + cross - targets[0].astype(F32)).astype(BF)

    pair = jnp.stack([err, permute(err, X_SWAP)])
    ups, downs = [pair], [pair]
    for _ in range(1, 4):
        ups.append(permute(ups[-1], Z_UP))
        downs.append(permute(downs[-1], Z_DOWN))
    far_same = permute(ups[-1][0], Z_UP)
    far_other = permute(downs[-1][1], Z_DOWN)
    carry = backprop(pos, [pair], (0,), codes_t, w)
    for hop in (1, 2, 3):
        carry = backprop(pos, [ups[hop], downs[hop]], (NZ - hop, hop), codes_t, w, carry)
    dec_grad, partial = backprop(pos, [far_same, far_other], (4,), codes_t, w, carry)

    halves = partial.reshape(8, 2, 32, 1024)
    core = tok % 2
    keep = lax.dynamic_index_in_dim(halves, core, 1, keepdims=False)
    give = lax.dynamic_index_in_dim(halves, 1 - core, 1, keepdims=False)
    chip = keep + permute(give, CORE_SWAP)
    shares = swap_blocks(chip.astype(BF), G_OUT).astype(F32)
    code_grad = jnp.sum(shares, axis=0)
    return code_grad[None], dec_grad.reshape(1, NL, 1024, 128)


def solution(mesh):
    return jax.shard_map(
        body,
        mesh=mesh,
        in_specs=(
            P("layer", "tok", None),
            P("layer", "tok", None),
            P("layer", None),
            P("layer", None, None, "tok"),
            P("layer", None, "tok"),
        ),
        out_specs=(P("layer", "tok", None), P("layer", None, None, "tok")),
        check_vma=False,
    )
```
